32 devices in a mesh: grp: 2 (over y), tile: 8 (over z, x), gene: 2 (over core).
Axes of the slice: x: 2, y: 2, z: 4, core: 2. Of those that a mesh axis runs over, the one named last changes fastest.
Arguments:
- counts: int32 [4096, 8192], P(('grp', 'tile'), 'gene'), parts along dimension 0, may hold values from 0 to 86, as said below
- cell_factor: float32 [32, 4096], P(None, ('grp', 'tile')), parts along dimension 1, may hold values from 0.05 to 1
- gene_factor: bfloat16 [32, 16384], P(None, ('grp', 'gene')), parts along dimension 1, may hold values from 0.049804688 to 1
- tissue: int32 [4096], P(('grp', 'tile')), parts along dimension 0, may hold values from 0 to 1, as said below
- neighbours: int32 [8, 4096], P(None, ('grp', 'tile')), parts along dimension 1, may hold values from 0 to 2047, as said below
Outputs:
- new_cells: float32 [32, 4096], P(None, ('grp', 'tile')), parts along dimension 1
- new_genes: bfloat16 [32, 16384], P(None, ('grp', 'gene')), parts along dimension 1
The draws below stay inside these ranges and needn't reach their ends.
There are 2 independent parts, one for each index of `grp`. The reference program is written for one: setup_inputs(seed, part) draws one part's arguments, and reference() takes and returns one part's arrays. A program takes and returns all parts, laid end to end along the dimension named above; each array names one. Nothing has to cross between parts.
Inputs may be any that keep to these rules, and one draw needn't show every extreme that they name: `counts`: counts of each cell and gene. Share of tissue differs among tiles. `neighbours`: every neighbour index lies within 32 positions of its cell in cell order, and that distance is reached.
All inputs are finite; a program needn't handle non-finite values.
Results may differ from the reference program's by a relative error of at most 0.00165.
Values may be sent and summed in bfloat16 or wider, within the bound.
A program may use at most 64 MiB of HBM per device.

```python
import math
import jax
import jax.numpy as jnp
from jax import lax

RANK = 32
GENES = 8192
C_DEV = 256
BORDER = 32
NEIGH = 8
PASSES = 2
CELLS = 2048
N_TILE = 8


def draw_counts(key, part):
    pair_key = jax.random.fold_in(key, 31)
    base_key = jax.random.fold_in(key, 32)
    extra_key = jax.random.fold_in(key, 33)
    tiles = CELLS // C_DEV
    block = GENES // tiles
    paired = jax.random.permutation(pair_key, tiles)
    target = paired[jnp.arange(CELLS, dtype=jnp.int32) // C_DEV]
    gene_block = jnp.arange(GENES, dtype=jnp.int32) // block
    hit = target[:, None] == gene_block[None, :]
    base = jax.random.randint(base_key, (CELLS, GENES), 0, 8)
    extra = jax.random.randint(extra_key, (CELLS, GENES), 48, 80)
    return (base + jnp.where(hit, extra, 0)).astype(jnp.int32)


def draw_tissue(key, part):
    level_key = jax.random.fold_in(key, 11)
    cell_key = jax.random.fold_in(key, 12)
    tiles = CELLS // C_DEV
    levels = jax.random.randint(level_key, (tiles,), 20, 96)
    per_cell = jnp.repeat(levels, C_DEV, total_repeat_length=CELLS)
    rolls = jax.random.randint(cell_key, (CELLS,), 0, 100)
    return (rolls < per_cell).astype(jnp.int32)


def draw_neighbours(key, part):
    step_key = jax.random.fold_in(key, 21)
    sign_key = jax.random.fold_in(key, 22)
    offsets = jax.random.randint(step_key, (NEIGH, CELLS), -BORDER, BORDER + 1)
    signs = 2 * jax.random.randint(sign_key, (1, CELLS), 0, 2) - 1
    first = signs * BORDER
    offsets = jnp.concatenate([first, offsets[1:]], axis=0)
    position = jnp.arange(CELLS, dtype=jnp.int32)[None, :]
    return jnp.clip(position + offsets, 0, CELLS - 1).astype(jnp.int32)


def block_levels(stream_key, dims, cuts, smallest, top_value):
    gain = 1.0
    for axis_at, parts in cuts:
        steps = jax.random.uniform(jax.random.fold_in(jax.random.fold_in(stream_key, 6), axis_at), (parts,), jnp.float32, smallest / len(cuts), top_value / len(cuts))
        gain = gain * jnp.repeat(jnp.exp(steps), dims[axis_at] // parts).reshape((-1,) + (1,) * (len(dims) - 1 - axis_at))
    return gain


def setup_inputs(seed: int = 0, part: int = 0) -> dict:
    key_list = jax.random.split(jax.random.key(seed), 6)
    part_keys = jax.random.split(jax.random.fold_in(key_list[5], part), 6)
    counts = draw_counts(jax.random.fold_in(jax.random.fold_in(key_list[5], part), 71), part)
    cell_factor = jnp.clip(jnp.exp(math.log(1.0) - 2.9957323 * jax.random.uniform(part_keys[1], (RANK, CELLS), jnp.float32) ** block_levels(part_keys[1], (RANK, CELLS), ((1, 8),), -0.2, 0.2)), 0.05, 1.0)
    gene_factor = jnp.clip(jnp.exp(math.log(1.0) - 2.9996462 * jax.random.uniform(part_keys[2], (RANK, GENES), jnp.float32) ** block_levels(part_keys[2], (RANK, GENES), ((1, 2),), -0.2, 0.2)), 0.049804688, 1.0).astype(jnp.bfloat16)
    tissue = draw_tissue(jax.random.fold_in(jax.random.fold_in(key_list[5], part), 71), part)
    neighbours = draw_neighbours(jax.random.fold_in(jax.random.fold_in(key_list[5], part), 71), part)
    return {"counts": counts, "cell_factor": cell_factor, "gene_factor": gene_factor, "tissue": tissue, "neighbours": neighbours}


smooth_weight = 0.5


def smooth(updated, tissue, neighbours):
    maskf = tissue.astype(jnp.float32)
    flat = neighbours.reshape(-1)
    count = neighbours.shape[0]
    near_mask = maskf[flat].reshape(count, CELLS)
    gathered = jnp.take(updated, flat, axis=1).reshape(RANK, count, CELLS)
    near = jnp.sum(gathered * near_mask[None], axis=1) / jnp.maximum(jnp.sum(near_mask, axis=0), 1.0)
    return jnp.where(tissue[None] > 0, (1.0 - smooth_weight) * updated + smooth_weight * near, updated)


def reference(counts, cell_factor, gene_factor, tissue, neighbours):
    hfull = gene_factor.astype(jnp.float32)
    maskf = tissue.astype(jnp.float32)
    gsum = jnp.sum(hfull, axis=1)
    blocks = jnp.arange(N_TILE, dtype=jnp.int32)

    def cell_numer(cells):
        def single(index):
            start = (index * C_DEV).astype(jnp.int32)
            wblock = lax.dynamic_slice_in_dim(cells, start, C_DEV, 1)
            xblock = lax.dynamic_slice_in_dim(counts, start, C_DEV, 0).astype(jnp.float32)
            product = lax.dot_general(wblock, hfull, (((0,), (0,)), ((), ())), precision=lax.Precision.HIGHEST)
            ratio = xblock / product
            return lax.dot_general(hfull, ratio, (((1,), (1,)), ((), ())), precision=lax.Precision.HIGHEST)
        pieces = lax.map(single, blocks)
        return jnp.transpose(pieces, (1, 0, 2)).reshape(RANK, CELLS)

    cells = cell_factor
    for step in range(PASSES):
        numer = cell_numer(cells)
        updated = jnp.where(tissue[None] > 0, cells * numer / gsum[:, None], cells)
        cells = smooth(updated, tissue, neighbours)

    def accumulate(total, index):
        start = (index * C_DEV).astype(jnp.int32)
        wblock = lax.dynamic_slice_in_dim(cells, start, C_DEV, 1)
        xblock = lax.dynamic_slice_in_dim(counts, start, C_DEV, 0).astype(jnp.float32)
        mblock = lax.dynamic_slice_in_dim(maskf, start, C_DEV, 0)
        product = lax.dot_general(wblock, hfull, (((0,), (0,)), ((), ())), precision=lax.Precision.HIGHEST)
        ratio = mblock[:, None] * xblock / product
        return total + jnp.dot(wblock, ratio, precision=lax.Precision.HIGHEST), None

    hnum, unused = lax.scan(accumulate, jnp.zeros((RANK, GENES), jnp.float32), blocks)
    hden = jnp.sum(cells * maskf[None], axis=1)
    new_genes = (hfull * hnum / hden[:, None]).astype(jnp.bfloat16)
    return cells, new_genes
```

```python
import functools

import jax
import jax.numpy as jnp
from jax import lax
from jax.experimental import pallas as pl
from jax.experimental.pallas import tpu as pltpu
from jax.sharding import PartitionSpec as P

BORDER = 32
PASSES = 2
LANES = 128
MESH = pl.DeviceIdType.MESH
WIRE = jnp.float32

smooth_weight = 0.5


def split(value):
    high = value.astype(jnp.bfloat16)
    low = (value - high.astype(jnp.float32)).astype(jnp.bfloat16)
    return high, low


def quotient(top, bottom):
    r = pl.reciprocal(bottom, approx=True)
    return top * (r * (2.0 - bottom * r))


def column_of(row, size):
    a = lax.broadcasted_iota(jnp.int32, (size, size), 0)
    b = lax.broadcasted_iota(jnp.int32, (size, size), 1)
    return jnp.sum(jnp.where(a == b, row, 0.0), axis=1, keepdims=True)


def kernel(
    n, owners, step,
    x_hbm, w_ref, h_ref, t_ref, nb_ref,
    cells_ref, genes_ref,
    x_ref, h2_ref, near_ref,
    nsend, nrecv, hrecv, wsend, wrecv, msend, mrecv,
    dsend, drecv, psend, precv, own_ref,
    x_sem, pair_s, pair_r, halo_s, halo_r, wb_s, wb_r, mb_s, mb_r,
    d_s, d_r, p_s, p_r, g_s, g_r,
):
    rank, width = w_ref.shape
    genes = h_ref.shape[1]
    chunk = genes // owners
    me = lax.axis_index("tile")
    core = lax.axis_index("gene")
    other = 1 - core
    barrier = pltpu.get_barrier_semaphore()

    loads = genes // step
    for c in range(loads):
        pltpu.make_async_copy(
            x_hbm.at[:, pl.ds(c * step, step)], x_ref.at[:, pl.ds(c * step, step)], x_sem.at[c]
        ).start()

    def greet(i, carry):
        peer = lax.rem(me + i, n)
        pl.semaphore_signal(barrier, inc=1, device_id={"tile": peer}, device_id_type=MESH)
        pl.semaphore_signal(
            barrier, inc=1, device_id={"tile": peer, "gene": other}, device_id_type=MESH
        )
        return carry

    lax.fori_loop(1, n, greet, 0)
    pl.semaphore_signal(barrier, inc=1, device_id={"gene": other}, device_id_type=MESH)

    h = h_ref[...]
    h2_ref[0:rank, :] = h
    h2_ref[rank : 2 * rank, :] = h
    gsum_part = lax.dot_general(
        jnp.ones((16, genes), jnp.bfloat16), h, (((1,), (1,)), ((), ())),
        preferred_element_type=jnp.float32,
    )[0:8]
    cells = jnp.transpose(w_ref[...])
    maskf = jnp.transpose(jnp.broadcast_to(t_ref[...].astype(jnp.float32), (8, width)))[:, 0:1]
    mask_w = jnp.broadcast_to(maskf, (width, rank))
    inside = mask_w > 0.0
    local = jnp.transpose((nb_ref[...] - (me * width - BORDER)).astype(jnp.float32))
    span = width + 2 * BORDER
    spot = lax.broadcasted_iota(jnp.int32, (width, span), 1).astype(jnp.float32)
    total = jnp.zeros((width, span), jnp.float32)
    for j in range(nb_ref.shape[0]):
        total = total + jnp.where(local[:, j : j + 1] == spot, 1.0, 0.0)
    near_ref[...] = total.astype(jnp.bfloat16)

    @pl.when(me == 0)
    def _():
        mrecv[0] = jnp.zeros((BORDER, rank), jnp.float32)
        for p in range(PASSES):
            wrecv[p, 0] = jnp.zeros((BORDER, rank), jnp.float32)
            for k in range(2):
                hrecv[p, 0, k] = jnp.zeros((BORDER, rank), jnp.float32)

    @pl.when(me == n - 1)
    def _():
        mrecv[1] = jnp.zeros((BORDER, rank), jnp.float32)
        for p in range(PASSES):
            wrecv[p, 1] = jnp.zeros((BORDER, rank), jnp.float32)
            for k in range(2):
                hrecv[p, 1, k] = jnp.zeros((BORDER, rank), jnp.float32)

    def to_sides(send, recv, ssem, rsem, gene):
        def make(side):
            peer = me + 1 if side == 0 else me - 1
            return pltpu.make_async_remote_copy(
                src_ref=send(side), dst_ref=recv(side), send_sem=ssem(side), recv_sem=rsem(side),
                device_id={"tile": peer, "gene": gene}, device_id_type=MESH,
            )
        return make

    ends = (width - BORDER, 0)

    def has(side):
        return me > 0 if side == 0 else me < n - 1

    def sends(side):
        return me < n - 1 if side == 0 else me > 0

    def w_copy(p):
        return to_sides(
            lambda s: wsend.at[p, s], lambda s: wrecv.at[p, s],
            lambda s: wb_s.at[p, s], lambda s: wb_r.at[p, s], core,
        )

    m_copy = to_sides(
        lambda s: msend.at[s], lambda s: mrecv.at[s],
        lambda s: mb_s.at[s], lambda s: mb_r.at[s], core,
    )

    def halo_copy(p, k):
        slot = core
        gene = core if k == 0 else other
        return to_sides(
            lambda s: nsend.at[p, pl.ds(ends[s], BORDER)], lambda s: hrecv.at[p, s, slot],
            lambda s: halo_s.at[p, s, k], lambda s: halo_r.at[p, s, slot], gene,
        )

    def halo_wait(p, side, slot):
        return pltpu.make_async_remote_copy(
            src_ref=nsend.at[p, pl.ds(ends[side], BORDER)], dst_ref=hrecv.at[p, side, slot],
            send_sem=halo_s.at[p, side, 0], recv_sem=halo_r.at[p, side, slot],
            device_id={"tile": lax.rem(me + 1, n)}, device_id_type=MESH,
        )

    def pair_copy(p):
        return pltpu.make_async_remote_copy(
            src_ref=nsend.at[p], dst_ref=nrecv.at[p], send_sem=pair_s.at[p], recv_sem=pair_r.at[p],
            device_id={"gene": other}, device_id_type=MESH,
        )

    def put_w(p, value):
        for side in range(2):
            wsend[p, side] = value[ends[side] : ends[side] + BORDER]

    for side in range(2):
        msend[side] = mask_w[ends[side] : ends[side] + BORDER]
    put_w(0, cells * mask_w)

    def ratio_of(w2, at, size):
        product = jnp.dot(w2, h2_ref[:, pl.ds(at, size)], preferred_element_type=jnp.float32)
        return quotient(x_ref[:, pl.ds(at, size)].astype(jnp.float32), product).astype(jnp.bfloat16)

    gsum = None
    for p in range(PASSES):
        w2 = jnp.concatenate(split(cells), axis=1)

        def body(c, acc, w2=w2, p=p):
            at = pl.multiple_of(c * step, step)
            if p == 0:
                pltpu.make_async_copy(
                    x_hbm.at[:, pl.ds(at, step)], x_ref.at[:, pl.ds(at, step)], x_sem.at[c]
                ).wait()
            ratio = ratio_of(w2, at, step)
            return acc + lax.dot_general(
                ratio, h_ref[:, pl.ds(at, step)], (((1,), (1,)), ((), ())),
                preferred_element_type=jnp.float32,
            )

        part = lax.fori_loop(0, loads, body, jnp.zeros((width, rank), jnp.float32))
        nsend[p, 0:width] = part
        nsend[p, width : width + 8] = gsum_part
        if p == 0:
            pl.semaphore_wait(barrier, 2 * (n - 1) + 1)
        for side in range(2):
            @pl.when(sends(side))
            def _():
                halo_copy(p, 0)(side).start()
                halo_copy(p, 1)(side).start()
                if p == 0:
                    w_copy(p)(side).start()
                    m_copy(side).start()
        pair_copy(p).start()
        pair_copy(p).wait_recv()
        numer = part + nrecv[p, 0:width]
        if gsum is None:
            gsum = gsum_part[0:1] + nrecv[p, width : width + 1]
            inverse = 1.0 / gsum
        updated = jnp.where(inside, cells * numer * inverse, cells)
        for side in range(2):
            @pl.when(has(side))
            def _():
                for k in range(2):
                    halo_wait(p, side, k).wait_recv()
                w_copy(p)(side).wait_recv()
                if p == 0:
                    m_copy(side).wait_recv()
        edges = []
        for side in range(2):
            edges.append(wrecv[p, side] * (hrecv[p, side, 0] + hrecv[p, side, 1]) * inverse)
        full = jnp.concatenate([edges[0], updated * mask_w, edges[1]], axis=0)
        masks = jnp.concatenate([mrecv[0], mask_w, mrecv[1]], axis=0).astype(jnp.bfloat16)
        stacked = jnp.concatenate(split(full) + (masks,), axis=1)
        mixed = jnp.dot(near_ref[...], stacked, preferred_element_type=jnp.float32)
        near = (mixed[:, 0:rank] + mixed[:, rank : 2 * rank]) / jnp.maximum(
            mixed[:, 2 * rank : 3 * rank], 1.0
        )
        cells = jnp.where(inside, (1.0 - smooth_weight) * updated + smooth_weight * near, updated)
        if p + 1 < PASSES:
            put_w(p + 1, cells * mask_w)
            for side in range(2):
                @pl.when(sends(side))
                def _():
                    w_copy(p + 1)(side).start()

    weighted = cells * mask_w
    dsend[...] = jnp.broadcast_to(jnp.sum(weighted, axis=0, keepdims=True), (8, rank))

    def den_copy(peer, source):
        return pltpu.make_async_remote_copy(
            src_ref=dsend, dst_ref=drecv.at[source], send_sem=d_s.at[peer], recv_sem=d_r.at[source],
            device_id={"tile": peer}, device_id_type=MESH,
        )

    def num_copy(peer, source):
        return pltpu.make_async_remote_copy(
            src_ref=psend.at[peer], dst_ref=precv.at[source], send_sem=p_s.at[peer],
            recv_sem=p_r.at[source], device_id={"tile": peer}, device_id_type=MESH,
        )

    def is_owner(index):
        return index < owners

    def den_start(i, carry):
        peer = lax.rem(me + i, n)
        @pl.when(is_owner(peer))
        def _():
            den_copy(peer, me).start()
        return carry

    lax.fori_loop(1, n, den_start, 0)
    w2 = jnp.concatenate(split(cells), axis=1)
    scale = 64.0 / width
    lift = jnp.concatenate(split(jnp.transpose(weighted) * scale), axis=0)

    def gene_part(owner):
        at = pl.multiple_of(owner * chunk, chunk)
        ratio = ratio_of(w2, at, chunk)
        both = jnp.dot(lift, ratio, preferred_element_type=jnp.float32)
        return (both[0:rank] + both[rank : 2 * rank]) * h_ref[:, pl.ds(at, chunk)].astype(jnp.float32)

    def num_start(i, carry):
        peer = lax.rem(me + i, n)
        @pl.when(is_owner(peer))
        def _():
            psend[peer] = gene_part(peer).astype(psend.dtype)
            num_copy(peer, me).start()
        return carry

    lax.fori_loop(1, n, num_start, 0)
    cells_ref[...] = jnp.transpose(cells)

    def gene_copy(peer, owner):
        at = pl.multiple_of(owner * chunk, chunk)
        return pltpu.make_async_remote_copy(
            src_ref=genes_ref.at[:, pl.ds(at, chunk)], dst_ref=genes_ref.at[:, pl.ds(at, chunk)],
            send_sem=g_s.at[peer], recv_sem=g_r.at[owner],
            device_id={"tile": peer}, device_id_type=MESH,
        )

    @pl.when(is_owner(me))
    def _():
        own_ref[...] = gene_part(me)

        def add(i, den):
            source = lax.rem(me + i, n)
            den_copy(source, source).wait_recv()
            num_copy(0, source).wait_recv()
            own_ref[...] = own_ref[...] + precv[source].astype(jnp.float32)
            return den + drecv[source]

        den = lax.fori_loop(1, n, add, dsend[...])
        inverse_den = column_of(1.0 / (den[0:1] * scale), rank)
        at = pl.multiple_of(me * chunk, chunk)
        genes_ref[:, pl.ds(at, chunk)] = (own_ref[...] * inverse_den).astype(genes_ref.dtype)

        def spread(i, carry):
            gene_copy(lax.rem(me + i, n), me).start()
            return carry

        lax.fori_loop(1, n, spread, 0)

    def finish(i, carry):
        peer = lax.rem(me + i, n)
        @pl.when(is_owner(peer))
        def _():
            gene_copy(peer, peer).wait_recv()
            den_copy(peer, me).wait_send()
            num_copy(peer, me).wait_send()
        @pl.when(is_owner(me))
        def _():
            gene_copy(peer, me).wait_send()
        return carry

    lax.fori_loop(1, n, finish, 0)
    for p in range(PASSES):
        pair_copy(p).wait_send()
        for side in range(2):
            @pl.when(sends(side))
            def _():
                halo_copy(p, 0)(side).wait_send()
                halo_copy(p, 1)(side).wait_send()
                w_copy(p)(side).wait_send()
                if p == 0:
                    m_copy(side).wait_send()


def on_device(n, counts, cell_factor, gene_factor, tissue, neighbours):
    width, genes = counts.shape
    rank = cell_factor.shape[0]
    owners = min(n, genes // LANES)
    step = min(512, genes)
    loads = genes // step
    chunk = genes // owners
    f32 = jnp.float32
    dma = pltpu.SemaphoreType.DMA
    vmem = pl.BlockSpec(memory_space=pltpu.VMEM)
    return pl.pallas_call(
        functools.partial(kernel, n, owners, step),
        out_shape=(
            jax.ShapeDtypeStruct((rank, width), f32),
            jax.ShapeDtypeStruct((rank, genes), jnp.bfloat16),
        ),
        in_specs=[pl.BlockSpec(memory_space=pl.ANY)] + [vmem] * 4,
        out_specs=(vmem, vmem),
        scratch_shapes=[
            pltpu.VMEM((width, genes), jnp.int32),
            pltpu.VMEM((2 * rank, genes), jnp.bfloat16),
            pltpu.VMEM((width, width + 2 * BORDER), jnp.bfloat16),
            pltpu.VMEM((PASSES, width + 8, rank), f32),
            pltpu.VMEM((PASSES, width + 8, rank), f32),
            pltpu.VMEM((PASSES, 2, 2, BORDER, rank), f32),
            pltpu.VMEM((PASSES, 2, BORDER, rank), f32),
            pltpu.VMEM((PASSES, 2, BORDER, rank), f32),
            pltpu.VMEM((2, BORDER, rank), f32),
            pltpu.VMEM((2, BORDER, rank), f32),
            pltpu.VMEM((8, rank), f32),
            pltpu.VMEM((n, 8, rank), f32),
            pltpu.VMEM((owners, rank, chunk), WIRE),
            pltpu.VMEM((n, rank, chunk), WIRE),
            pltpu.VMEM((rank, chunk), f32),
            dma((loads,)),
            dma((PASSES,)),
            dma((PASSES,)),
            dma((PASSES, 2, 2)),
            dma((PASSES, 2, 2)),
            dma((PASSES, 2)),
            dma((PASSES, 2)),
            dma((2,)),
            dma((2,)),
            dma((n,)),
            dma((n,)),
            dma((n,)),
            dma((n,)),
            dma((n,)),
            dma((n,)),
        ],
        compiler_params=pltpu.CompilerParams(collective_id=0, has_side_effects=True),
    )(counts, cell_factor, gene_factor, tissue.reshape(1, width), neighbours)


def solution(mesh):
    return jax.shard_map(
        functools.partial(on_device, mesh.shape["tile"]),
        mesh=mesh,
        in_specs=(
            P(("grp", "tile"), "gene"),
            P(None, ("grp", "tile")),
            P(None, ("grp", "gene")),
            P(("grp", "tile")),
            P(None, ("grp", "tile")),
        ),
        out_specs=(P(None, ("grp", "tile")), P(None, ("grp", "gene"))),
        check_vma=False,
    )
```

```python
import functools

import jax
import jax.numpy as jnp
from jax import lax
from jax.experimental import pallas as pl
from jax.experimental.pallas import tpu as pltpu
from jax.sharding import PartitionSpec as P

BORDER = 32
PASSES = 2
LANES = 128
MESH = pl.DeviceIdType.MESH
WIRE = jnp.int16
TOP = 32000.0

smooth_weight = 0.5


def split(value):
    high = value.astype(jnp.bfloat16)
    low = (value - high.astype(jnp.float32)).astype(jnp.bfloat16)
    return high, low


def quotient(top, bottom):
    r = pl.reciprocal(bottom, approx=True)
    return top * (r * (2.0 - bottom * r))


def column_of(row, size):
    a = lax.broadcasted_iota(jnp.int32, (size, size), 0)
    b = lax.broadcasted_iota(jnp.int32, (size, size), 1)
    return jnp.sum(jnp.where(a == b, row, 0.0), axis=1, keepdims=True)


def row_of(column, size):
    a = lax.broadcasted_iota(jnp.int32, (size, size), 0)
    b = lax.broadcasted_iota(jnp.int32, (size, size), 1)
    return jnp.sum(jnp.where(a == b, column, 0.0), axis=0, keepdims=True)


def encode(part, wire, unit):
    rank = part.shape[0]
    top = jnp.maximum(jnp.max(part, axis=1, keepdims=True), 1e-30)
    wire[...] = (part * (TOP / top) + 0.5).astype(jnp.int32).astype(WIRE)
    unit[...] = jnp.broadcast_to(row_of(top * (1.0 / TOP), rank), unit.shape)


def decode(wire, unit):
    rank = wire.shape[0]
    return wire[...].astype(jnp.int32).astype(jnp.float32) * column_of(unit[0:1], rank)


def kernel(
    n, owners, step,
    x_hbm, w_ref, h_ref, t_ref, nb_ref,
    cells_ref, genes_ref,
    x_ref, h2_ref, near_ref,
    nsend, nrecv, hrecv, wsend, wrecv, msend, mrecv,
    dsend, drecv, psend, precv, usend, urecv, qsend, qrecv, vsend, vrecv, own_ref,
    x_sem, pair_s, pair_r, halo_s, halo_r, wb_s, wb_r, mb_s, mb_r,
    d_s, d_r, p_s, p_r, q_s, q_r, g_s, g_r, f_s, f_r,
):
    rank, width = w_ref.shape
    genes = h_ref.shape[1]
    chunk = genes // owners
    me = lax.axis_index("tile")
    core = lax.axis_index("gene")
    other = 1 - core
    barrier = pltpu.get_barrier_semaphore()

    loads = genes // step
    for c in range(loads):
        pltpu.make_async_copy(
            x_hbm.at[:, pl.ds(c * step, step)], x_ref.at[:, pl.ds(c * step, step)], x_sem.at[c]
        ).start()

    def greet(i, carry):
        peer = lax.rem(me + i, n)
        pl.semaphore_signal(barrier, inc=1, device_id={"tile": peer}, device_id_type=MESH)
        pl.semaphore_signal(
            barrier, inc=1, device_id={"tile": peer, "gene": other}, device_id_type=MESH
        )
        return carry

    lax.fori_loop(1, n, greet, 0)
    pl.semaphore_signal(barrier, inc=1, device_id={"gene": other}, device_id_type=MESH)

    h = h_ref[...]
    h2_ref[0:rank, :] = h
    h2_ref[rank : 2 * rank, :] = h
    gsum_part = lax.dot_general(
        jnp.ones((16, genes), jnp.bfloat16), h, (((1,), (1,)), ((), ())),
        preferred_element_type=jnp.float32,
    )[0:8]
    cells = jnp.transpose(w_ref[...])
    maskf = jnp.transpose(jnp.broadcast_to(t_ref[...].astype(jnp.float32), (8, width)))[:, 0:1]
    mask_w = jnp.broadcast_to(maskf, (width, rank))
    inside = mask_w > 0.0
    local = jnp.transpose((nb_ref[...] - (me * width - BORDER)).astype(jnp.float32))
    span = width + 2 * BORDER
    spot = lax.broadcasted_iota(jnp.int32, (width, span), 1).astype(jnp.float32)
    total = jnp.zeros((width, span), jnp.float32)
    for j in range(nb_ref.shape[0]):
        total = total + jnp.where(local[:, j : j + 1] == spot, 1.0, 0.0)
    near_ref[...] = total.astype(jnp.bfloat16)

    @pl.when(me == 0)
    def _():
        mrecv[0] = jnp.zeros((BORDER, rank), jnp.float32)
        for p in range(PASSES):
            wrecv[p, 0] = jnp.zeros((BORDER, rank), jnp.float32)
            for k in range(2):
                hrecv[p, 0, k] = jnp.zeros((BORDER, rank), jnp.float32)

    @pl.when(me == n - 1)
    def _():
        mrecv[1] = jnp.zeros((BORDER, rank), jnp.float32)
        for p in range(PASSES):
            wrecv[p, 1] = jnp.zeros((BORDER, rank), jnp.float32)
            for k in range(2):
                hrecv[p, 1, k] = jnp.zeros((BORDER, rank), jnp.float32)

    def to_sides(send, recv, ssem, rsem, gene):
        def make(side):
            peer = me + 1 if side == 0 else me - 1
            return pltpu.make_async_remote_copy(
                src_ref=send(side), dst_ref=recv(side), send_sem=ssem(side), recv_sem=rsem(side),
                device_id={"tile": peer, "gene": gene}, device_id_type=MESH,
            )
        return make

    ends = (width - BORDER, 0)

    def has(side):
        return me > 0 if side == 0 else me < n - 1

    def sends(side):
        return me < n - 1 if side == 0 else me > 0

    def w_copy(p):
        return to_sides(
            lambda s: wsend.at[p, s], lambda s: wrecv.at[p, s],
            lambda s: wb_s.at[p, s], lambda s: wb_r.at[p, s], core,
        )

    m_copy = to_sides(
        lambda s: msend.at[s], lambda s: mrecv.at[s],
        lambda s: mb_s.at[s], lambda s: mb_r.at[s], core,
    )

    def halo_copy(p, k):
        slot = core
        gene = core if k == 0 else other
        return to_sides(
            lambda s: nsend.at[p, pl.ds(ends[s], BORDER)], lambda s: hrecv.at[p, s, slot],
            lambda s: halo_s.at[p, s, k], lambda s: halo_r.at[p, s, slot], gene,
        )

    def halo_wait(p, side, slot):
        return pltpu.make_async_remote_copy(
            src_ref=nsend.at[p, pl.ds(ends[side], BORDER)], dst_ref=hrecv.at[p, side, slot],
            send_sem=halo_s.at[p, side, 0], recv_sem=halo_r.at[p, side, slot],
            device_id={"tile": lax.rem(me + 1, n)}, device_id_type=MESH,
        )

    def pair_copy(p):
        return pltpu.make_async_remote_copy(
            src_ref=nsend.at[p], dst_ref=nrecv.at[p], send_sem=pair_s.at[p], recv_sem=pair_r.at[p],
            device_id={"gene": other}, device_id_type=MESH,
        )

    def put_w(p, value):
        for side in range(2):
            wsend[p, side] = value[ends[side] : ends[side] + BORDER]

    for side in range(2):
        msend[side] = mask_w[ends[side] : ends[side] + BORDER]
    put_w(0, cells * mask_w)

    def ratio_of(w2, at, size):
        product = jnp.dot(w2, h2_ref[:, pl.ds(at, size)], preferred_element_type=jnp.float32)
        return quotient(x_ref[:, pl.ds(at, size)].astype(jnp.float32), product).astype(jnp.bfloat16)

    gsum = None
    for p in range(PASSES):
        w2 = jnp.concatenate(split(cells), axis=1)

        def body(c, acc, w2=w2, p=p):
            at = pl.multiple_of(c * step, step)
            if p == 0:
                pltpu.make_async_copy(
                    x_hbm.at[:, pl.ds(at, step)], x_ref.at[:, pl.ds(at, step)], x_sem.at[c]
                ).wait()
            ratio = ratio_of(w2, at, step)
            return acc + lax.dot_general(
                ratio, h_ref[:, pl.ds(at, step)], (((1,), (1,)), ((), ())),
                preferred_element_type=jnp.float32,
            )

        part = lax.fori_loop(0, loads, body, jnp.zeros((width, rank), jnp.float32))
        nsend[p, 0:width] = part
        nsend[p, width : width + 8] = gsum_part
        if p == 0:
            pl.semaphore_wait(barrier, 2 * (n - 1) + 1)
        for side in range(2):
            @pl.when(sends(side))
            def _():
                halo_copy(p, 0)(side).start()
                halo_copy(p, 1)(side).start()
                if p == 0:
                    w_copy(p)(side).start()
                    m_copy(side).start()
        pair_copy(p).start()
        pair_copy(p).wait_recv()
        numer = part + nrecv[p, 0:width]
        if gsum is None:
            gsum = gsum_part[0:1] + nrecv[p, width : width + 1]
            inverse = 1.0 / gsum
        updated = jnp.where(inside, cells * numer * inverse, cells)
        for side in range(2):
            @pl.when(has(side))
            def _():
                for k in range(2):
                    halo_wait(p, side, k).wait_recv()
                w_copy(p)(side).wait_recv()
                if p == 0:
                    m_copy(side).wait_recv()
        edges = []
        for side in range(2):
            edges.append(wrecv[p, side] * (hrecv[p, side, 0] + hrecv[p, side, 1]) * inverse)
        full = jnp.concatenate([edges[0], updated * mask_w, edges[1]], axis=0)
        masks = jnp.concatenate([mrecv[0], mask_w, mrecv[1]], axis=0).astype(jnp.bfloat16)
        stacked = jnp.concatenate(split(full) + (masks,), axis=1)
        mixed = jnp.dot(near_ref[...], stacked, preferred_element_type=jnp.float32)
        near = (mixed[:, 0:rank] + mixed[:, rank : 2 * rank]) / jnp.maximum(
            mixed[:, 2 * rank : 3 * rank], 1.0
        )
        cells = jnp.where(inside, (1.0 - smooth_weight) * updated + smooth_weight * near, updated)
        if p + 1 < PASSES:
            put_w(p + 1, cells * mask_w)
            for side in range(2):
                @pl.when(sends(side))
                def _():
                    w_copy(p + 1)(side).start()

    weighted = cells * mask_w
    dsend[...] = jnp.broadcast_to(jnp.sum(weighted, axis=0, keepdims=True), (8, rank))

    def den_copy(peer, source):
        return pltpu.make_async_remote_copy(
            src_ref=dsend, dst_ref=drecv.at[source], send_sem=d_s.at[peer], recv_sem=d_r.at[source],
            device_id={"tile": peer}, device_id_type=MESH,
        )

    def is_owner(index):
        return index < owners

    def den_start(i, carry):
        peer = lax.rem(me + i, n)
        @pl.when(is_owner(peer))
        def _():
            den_copy(peer, me).start()
        return carry

    lax.fori_loop(1, n, den_start, 0)
    w2 = jnp.concatenate(split(cells), axis=1)
    lift = jnp.concatenate(split(jnp.transpose(weighted)), axis=0)
    outers = n // 2
    zi, xi = me // 2, lax.rem(me, 2)
    mate = zi * 2 + 1 - xi

    def gene_part(owner):
        at = pl.multiple_of(owner * chunk, chunk)
        ratio = ratio_of(w2, at, chunk)
        both = jnp.dot(lift, ratio, preferred_element_type=jnp.float32)
        return both[0:rank] + both[rank : 2 * rank]

    def move(src, dst, ssem, rsem, tile):
        return pltpu.make_async_remote_copy(
            src_ref=src, dst_ref=dst, send_sem=ssem, recv_sem=rsem,
            device_id={"tile": tile}, device_id_type=MESH,
        )

    def first(z):
        return (
            move(psend.at[z], precv.at[z], p_s.at[0, z], p_r.at[0, z], mate),
            move(usend.at[z], urecv.at[z], p_s.at[1, z], p_r.at[1, z], mate),
        )

    def second(z, source):
        return (
            move(qsend.at[z], qrecv.at[source], q_s.at[0, z], q_r.at[0, source], 2 * z + xi),
            move(vsend.at[z], vrecv.at[source], q_s.at[1, z], q_r.at[1, source], 2 * z + xi),
        )

    def place(z, x):
        return genes_ref.at[:, pl.ds(pl.multiple_of((2 * z + x) * chunk, chunk), chunk)]

    def along(z, source):
        return move(place(source, xi), place(source, xi), g_s.at[z], g_r.at[source], 2 * z + xi)

    def across(z, x):
        return move(place(z, x), place(z, x), f_s.at[z], f_r.at[z], mate)

    def turn(i):
        return lax.rem(zi + i, outers)

    def first_start(i, carry):
        z = turn(i)
        @pl.when(is_owner(2 * z))
        def _():
            encode(gene_part(2 * z + 1 - xi), psend.at[z], usend.at[z])
            for copy in first(z):
                copy.start()
        return carry

    lax.fori_loop(1, outers + 1, first_start, 0)

    def second_start(i, carry):
        z = turn(i)
        @pl.when(is_owner(2 * z))
        def _():
            part = gene_part(2 * z + xi)
            for copy in first(z):
                copy.wait_recv()
            part = part + decode(precv.at[z], urecv.at[z])
            @pl.when(z != zi)
            def _():
                encode(part, qsend.at[z], vsend.at[z])
                for copy in second(z, zi):
                    copy.start()
            @pl.when(z == zi)
            def _():
                own_ref[...] = part
        return carry

    lax.fori_loop(1, outers + 1, second_start, 0)
    cells_ref[...] = jnp.transpose(cells)

    @pl.when(is_owner(me))
    def _():
        def add_den(i, den):
            source = lax.rem(me + i, n)
            den_copy(source, source).wait_recv()
            return den + drecv[source]

        den = lax.fori_loop(1, n, add_den, dsend[...])
        inverse_den = column_of(1.0 / den[0:1], rank)
        at = pl.multiple_of(me * chunk, chunk)
        lead = h_ref[:, pl.ds(at, chunk)].astype(jnp.float32) * inverse_den

        def add(i, total):
            source = turn(i)
            for copy in second(source, source):
                copy.wait_recv()
            return total + decode(qrecv.at[source], vrecv.at[source])

        total = lax.fori_loop(1, outers, add, own_ref[...])
        genes_ref[:, pl.ds(at, chunk)] = (lead * total).astype(genes_ref.dtype)

        def spread(i, carry):
            along(turn(i), zi).start()
            return carry

        lax.fori_loop(1, outers, spread, 0)
        across(zi, xi).start()

    def forward(i, carry):
        z = turn(i)
        @pl.when(is_owner(2 * z))
        def _():
            along(z, z).wait_recv()
            across(z, xi).start()
        return carry

    lax.fori_loop(1, outers, forward, 0)

    def finish(i, carry):
        z = turn(i)
        @pl.when(is_owner(2 * z))
        def _():
            across(z, 1 - xi).wait_recv()
            across(z, xi).wait_send()
            for copy in first(z):
                copy.wait_send()
            @pl.when(z != zi)
            def _():
                for copy in second(z, zi):
                    copy.wait_send()
        @pl.when((z != zi) & is_owner(me))
        def _():
            along(z, zi).wait_send()
        return carry

    lax.fori_loop(1, outers + 1, finish, 0)

    def den_finish(i, carry):
        peer = lax.rem(me + i, n)
        @pl.when(is_owner(peer))
        def _():
            den_copy(peer, me).wait_send()
        return carry

    lax.fori_loop(1, n, den_finish, 0)
    for p in range(PASSES):
        pair_copy(p).wait_send()
        for side in range(2):
            @pl.when(sends(side))
            def _():
                halo_copy(p, 0)(side).wait_send()
                halo_copy(p, 1)(side).wait_send()
                w_copy(p)(side).wait_send()
                if p == 0:
                    m_copy(side).wait_send()


def settle(cells_in, genes_in, cells_ref, genes_ref):
    cells_ref[...] = cells_in[...]
    genes_ref[...] = genes_in[...]


def on_device(n, counts, cell_factor, gene_factor, tissue, neighbours):
    width, genes = counts.shape
    rank = cell_factor.shape[0]
    owners = min(n, genes // LANES)
    step = min(512, genes)
    loads = genes // step
    chunk = genes // owners
    f32 = jnp.float32
    dma = pltpu.SemaphoreType.DMA
    vmem = pl.BlockSpec(memory_space=pltpu.VMEM)
    shapes = (
        jax.ShapeDtypeStruct((rank, width), f32),
        jax.ShapeDtypeStruct((rank, genes), jnp.bfloat16),
    )
    results = pl.pallas_call(
        functools.partial(kernel, n, owners, step),
        out_shape=shapes,
        in_specs=[pl.BlockSpec(memory_space=pl.ANY)] + [vmem] * 4,
        out_specs=(vmem, vmem),
        scratch_shapes=[
            pltpu.VMEM((width, genes), jnp.int32),
            pltpu.VMEM((2 * rank, genes), jnp.bfloat16),
            pltpu.VMEM((width, width + 2 * BORDER), jnp.bfloat16),
            pltpu.VMEM((PASSES, width + 8, rank), f32),
            pltpu.VMEM((PASSES, width + 8, rank), f32),
            pltpu.VMEM((PASSES, 2, 2, BORDER, rank), f32),
            pltpu.VMEM((PASSES, 2, BORDER, rank), f32),
            pltpu.VMEM((PASSES, 2, BORDER, rank), f32),
            pltpu.VMEM((2, BORDER, rank), f32),
            pltpu.VMEM((2, BORDER, rank), f32),
            pltpu.VMEM((8, rank), f32),
            pltpu.VMEM((n, 8, rank), f32),
            pltpu.VMEM((owners // 2, rank, chunk), WIRE),
            pltpu.VMEM((owners // 2, rank, chunk), WIRE),
            pltpu.VMEM((owners // 2, 8, rank), f32),
            pltpu.VMEM((owners // 2, 8, rank), f32),
            pltpu.VMEM((owners // 2, rank, chunk), WIRE),
            pltpu.VMEM((n // 2, rank, chunk), WIRE),
            pltpu.VMEM((owners // 2, 8, rank), f32),
            pltpu.VMEM((n // 2, 8, rank), f32),
            pltpu.VMEM((rank, chunk), f32),
            dma((loads,)),
            dma((PASSES,)),
            dma((PASSES,)),
            dma((PASSES, 2, 2)),
            dma((PASSES, 2, 2)),
            dma((PASSES, 2)),
            dma((PASSES, 2)),
            dma((2,)),
            dma((2,)),
            dma((n,)),
            dma((n,)),
            dma((2, n // 2)),
            dma((2, n // 2)),
            dma((2, n // 2)),
            dma((2, n // 2)),
            dma((n // 2,)),
            dma((n // 2,)),
            dma((n // 2,)),
            dma((n // 2,)),
        ],
        compiler_params=pltpu.CompilerParams(collective_id=0, has_side_effects=True),
    )(counts, cell_factor, gene_factor, tissue.reshape(1, width), neighbours)
    return pl.pallas_call(
        settle, out_shape=shapes, in_specs=[vmem] * 2, out_specs=(vmem, vmem)
    )(*results)


def solution(mesh):
    return jax.shard_map(
        functools.partial(on_device, mesh.shape["tile"]),
        mesh=mesh,
        in_specs=(
            P(("grp", "tile"), "gene"),
            P(None, ("grp", "tile")),
            P(None, ("grp", "gene")),
            P(("grp", "tile")),
            P(None, ("grp", "tile")),
        ),
        out_specs=(P(None, ("grp", "tile")), P(None, ("grp", "gene"))),
        check_vma=False,
    )
```
